512 devices in a mesh: row: 32 (over y, x), col: 16 (over z, core).
Axes of the slice: x: 4, y: 8, z: 8, core: 2. Of those that a mesh axis runs over, the one named last changes fastest.
Arguments:
- activations: bfloat16 [384, 8192], P('row', 'col'), may hold values from -6 to 6
- gate_weight: bfloat16 [8192, 16384], P('col', 'row'), may hold values from -0.0625 to 0.0625
- up_weight: bfloat16 [8192, 16384], P('col', 'row'), may hold values from -0.0625 to 0.0625
- down_weight: bfloat16 [16384, 8192], P('row', 'col'), may hold values from -0.046875 to 0.046875
- out_grad: bfloat16 [384, 8192], P('row', 'col'), may hold values from -1.75 to 1.75
Outputs:
- layer_out: bfloat16 [384, 8192], P('row', 'col')
- input_grad: bfloat16 [384, 8192], P('row', 'col')
- gate_grad: float32 [8192, 16384], P('col', 'row')
- up_grad: float32 [8192, 16384], P('col', 'row')
- down_grad: float32 [16384, 8192], P('row', 'col')
The draws below stay inside these ranges and needn't reach their ends.
All inputs are finite; a program needn't handle non-finite values.
Results may differ from the reference program's by a relative error of at most 0.005.
Values may be sent and summed in bfloat16 or wider, within the bound.
No kernel may reach another device: no remote copies, remote signals or barrier semaphores. Data moves between devices by JAX's collectives and lax.ppermute only.
A program may use at most 64 MiB of HBM per device.

```python
import jax
import jax.numpy as jnp
from jax import lax

D = 8192
F = 16384
TOKENS = 384


def block_scale(key, shape, pieces, low, high):
    loudness, own = 1.0, jax.random.fold_in(key, 6)
    for axis_at, blocks in pieces:
        draws = jnp.exp(jax.random.uniform(jax.random.fold_in(own, axis_at), (blocks,), jnp.float32, low / len(pieces), high / len(pieces)))
        loudness = loudness * jnp.repeat(draws, shape[axis_at] // blocks).reshape([-1 if axis == axis_at else 1 for axis in range(len(shape))])
    return loudness


def normal_values(own_key, extent, spread, most, cuts=(), held_as=jnp.bfloat16):
    result = jax.random.normal(own_key, extent, jnp.float32) * spread
    if len(cuts) > 0:
        result = block_scale(own_key, extent, cuts, -0.22, 0.18) * result
    return jnp.clip(result, min=-most, max=most).astype(held_as)


def setup_inputs(seed: int = 0) -> dict:
    arg_keys = jax.random.split(jax.random.key(seed), 6)
    activations = normal_values(arg_keys[0], (TOKENS, D), 1.0, 6.0, ((0, 32), (1, 16)))
    gate_weight = normal_values(arg_keys[1], (D, F), D ** -0.5, 0.0625, ((0, 16), (1, 32)))
    up_weight = normal_values(arg_keys[2], (D, F), D ** -0.5, 0.0625, ((0, 16), (1, 32)))
    down_weight = normal_values(arg_keys[3], (F, D), F ** -0.5, 0.046875, ((0, 32), (1, 16)))
    out_grad = normal_values(arg_keys[4], (TOKENS, D), 0.3, 1.75, ((0, 32), (1, 16)))
    return dict(activations=activations, gate_weight=gate_weight, up_weight=up_weight, down_weight=down_weight, out_grad=out_grad)


def contract_cols(left_side, right_side):
    return lax.dot_general(left_side, right_side, (((1,), (1,)), ((), ())), preferred_element_type=jnp.float32)


def swiglu_deltas(hidden_grad, gate, up):
    gate_sigmoid = jax.nn.sigmoid(gate)
    gate_silu = gate * gate_sigmoid
    gate_delta = (hidden_grad * up * gate_sigmoid * (1.0 + gate * (1.0 - gate_sigmoid))).astype(jnp.bfloat16)
    up_delta = (hidden_grad * gate_silu).astype(jnp.bfloat16)
    return gate_delta, up_delta


def reference(activations, gate_weight, up_weight, down_weight, out_grad):
    gate = jnp.dot(activations, gate_weight, preferred_element_type=jnp.float32)
    up = jnp.dot(activations, up_weight, preferred_element_type=jnp.float32)
    hidden = (jax.nn.silu(gate) * up).astype(jnp.bfloat16)
    layer_out = jnp.dot(hidden, down_weight, preferred_element_type=jnp.float32).astype(jnp.bfloat16)
    hidden_grad = contract_cols(out_grad, down_weight)
    gate_delta, up_delta = swiglu_deltas(hidden_grad, gate, up)
    gate_grad = jnp.dot(activations.T, gate_delta, preferred_element_type=jnp.float32)
    up_grad = jnp.dot(activations.T, up_delta, preferred_element_type=jnp.float32)
    down_grad = jnp.dot(hidden.T, out_grad, preferred_element_type=jnp.float32)
    input_grad = (contract_cols(gate_delta, gate_weight) + contract_cols(up_delta, up_weight)).astype(jnp.bfloat16)
    return (layer_out, input_grad, gate_grad, up_grad, down_grad)
```

```python
import functools

import jax
import jax.numpy as jnp
from jax import lax
from jax.experimental import pallas as pl
from jax.experimental.pallas import tpu as pltpu
from jax.sharding import Mesh, PartitionSpec as P

F32 = jnp.float32
BF16 = jnp.bfloat16
VM = pl.BlockSpec(memory_space=pltpu.VMEM)
SM = pl.BlockSpec(memory_space=pltpu.SMEM)
PARAMS = pltpu.CompilerParams(vmem_limit_bytes=40 * 2**20)


def mm(left, right):
    return jnp.dot(left, right, preferred_element_type=F32)


def mm_t(left, right):
    return lax.dot_general(left, right, (((1,), (1,)), ((), ())), preferred_element_type=F32)


def t_mm(left, right):
    return lax.dot_general(left, right, (((0,), (0,)), ((), ())), preferred_element_type=F32)


def spread(block, axis, size):
    return lax.all_to_all(jnp.broadcast_to(block[None], (size,) + block.shape), axis, 0, 0)


def add_up(blocks):
    total = blocks[0].astype(F32)
    for i in range(1, blocks.shape[0]):
        total = total + blocks[i].astype(F32)
    return total


def low_rows(shape):
    return lax.broadcasted_iota(jnp.int32, shape, 1) < 4


def pack_kernel(a, b, out):
    head = (a[:8], b[:8])
    tail = jnp.concatenate([a[8:].astype(F32), b[8:].astype(F32)], axis=0).astype(BF16)
    for i in range(out.shape[0]):
        out[i, 0:8, :] = head[0]
        out[i, 8:16, :] = head[1]
        out[i, 16:24, :] = tail


def pack(a, b, copies):
    return pl.pallas_call(
        pack_kernel,
        out_shape=jax.ShapeDtypeStruct((copies, 24, a.shape[1]), BF16),
        in_specs=[VM, VM],
        out_specs=VM,
        compiler_params=PARAMS,
        name="pack",
    )(a, b)


def total_kernel(blocks, layer_out, input_grad):
    total = blocks[0].astype(F32)
    for i in range(1, blocks.shape[0]):
        total = total + blocks[i].astype(F32)
    layer_out[:8] = total[:8].astype(BF16)
    layer_out[8:] = total[16:20].astype(BF16)
    input_grad[:8] = total[8:16].astype(BF16)
    input_grad[8:] = total[20:24].astype(BF16)


def totals(blocks):
    shape = jax.ShapeDtypeStruct((12, blocks.shape[2]), BF16)
    return pl.pallas_call(total_kernel, out_shape=(shape, shape), in_specs=[VM], compiler_params=PARAMS, name="totals")(blocks)


def partial_kernel(which, blocks, gate_weight, up_weight, down_weight, out, x_out, g_out):
    m = x_out.shape[0] // 12
    d = x_out.shape[1]
    rows = pl.ds(which[0] * m, m)
    tail = blocks[rows, 16:24, :].astype(F32).reshape(m // 2, 16, d)
    even, odd = tail[:, :8], tail[:, 8:]
    low = low_rows(even.shape)
    x_tail = jnp.where(low, even, pltpu.roll(odd, 4, 1)).reshape(m * 4, d)
    g_tail = jnp.where(low, pltpu.roll(even, 4, 1), odd).reshape(m * 4, d)
    x_head = blocks[rows, 0:8, :].astype(F32).reshape(m * 8, d)
    g_head = blocks[rows, 8:16, :].astype(F32).reshape(m * 8, d)
    x = jnp.concatenate([x_head, x_tail], axis=0).astype(BF16)
    g = jnp.concatenate([g_head, g_tail], axis=0).astype(BF16)
    x_out[...] = x
    g_out[...] = g
    h = gate_weight.shape[1]
    out[:, :h] = mm(x, gate_weight[...])
    out[:, h : 2 * h] = mm(x, up_weight[...])
    out[:, 2 * h :] = mm_t(g, down_weight[...])


def partial_sums(which, blocks, gate_weight, up_weight, down_weight):
    n = blocks.shape[0] * 12 // 2
    d = blocks.shape[2]
    h = gate_weight.shape[1]
    shape = jax.ShapeDtypeStruct
    return pl.pallas_call(
        partial_kernel,
        out_shape=(shape((n, 3 * h), F32), shape((n, d), BF16), shape((n, d), BF16)),
        in_specs=[SM, VM, VM, VM, VM],
        out_specs=(VM, VM, VM),
        compiler_params=PARAMS,
        cost_estimate=pl.CostEstimate(flops=2 * n * d * 3 * h, bytes_accessed=4 * n * 3 * h, transcendentals=0),
        name="partial_sums",
    )(which, blocks, gate_weight, up_weight, down_weight)


def output_kernel(which, own, other, gate_weight, up_weight, down_weight, out):
    h = gate_weight.shape[1]
    d = gate_weight.shape[0]
    for part, where in ((own, which[0]), (other, 1 - which[0])):
        m = part.shape[0] // 12
        f = mm(part[:, :h], down_weight[...])
        b = mm_t(part[:, h : 2 * h], gate_weight[...]) + mm_t(part[:, 2 * h :], up_weight[...])
        rows = pl.ds(where * m, m)
        out[rows, 0:8, :] = f[: m * 8].reshape(m, 8, d).astype(BF16)
        out[rows, 8:16, :] = b[: m * 8].reshape(m, 8, d).astype(BF16)
        f = f[m * 8 :].reshape(m // 2, 8, d)
        b = b[m * 8 :].reshape(m // 2, 8, d)
        low = low_rows(f.shape)
        even = jnp.where(low, f, pltpu.roll(b, 4, 1))
        odd = jnp.where(low, pltpu.roll(f, 4, 1), b)
        out[rows, 16:24, :] = jnp.concatenate([even, odd], axis=1).reshape(m, 8, d).astype(BF16)


def output_blocks(which, own, other, gate_weight, up_weight, down_weight):
    n, width = own.shape
    d = gate_weight.shape[0]
    return pl.pallas_call(
        output_kernel,
        out_shape=jax.ShapeDtypeStruct((n // 6, 24, d), BF16),
        in_specs=[SM, VM, VM, VM, VM, VM],
        out_specs=VM,
        compiler_params=PARAMS,
        cost_estimate=pl.CostEstimate(flops=4 * n * d * width, bytes_accessed=8 * n * d, transcendentals=0),
        name="output_blocks",
    )(which, own, other, gate_weight, up_weight, down_weight)


def local(sizes, activations, gate_weight, up_weight, down_weight, out_grad):
    ny, nx, nz, nc = sizes
    d = activations.shape[1]
    h = gate_weight.shape[1]
    rows = ny * nx
    swap = [(0, 1), (1, 0)]
    core = lax.axis_index("core").astype(jnp.int32).reshape(1)
    away = 1 - core

    both = pack(activations, out_grad, ny)
    both, core, away = lax.optimization_barrier((both, core, away))
    both = spread(lax.all_to_all(both, "y", 0, 0), "x", nx).reshape(rows, 24, d)
    weights = (gate_weight, up_weight, down_weight)
    send, x_other, g_other = partial_sums(away, both, *weights)
    sent = lax.ppermute(send, "core", swap)
    keep, x_own, g_own = partial_sums(core, both, *weights)
    half = keep.shape[0]
    n = half // nz
    chip = (keep + sent).astype(BF16).reshape(nz, n, 3 * h)
    summed = add_up(lax.all_to_all(chip, "z", 0, 0))
    gate, up, hidden_grad = summed[:, :h], summed[:, h : 2 * h], summed[:, 2 * h :]
    sig = jax.nn.sigmoid(gate)
    silu = gate * sig
    hidden = (silu * up).astype(BF16)
    gate_delta = (hidden_grad * up * sig * (1.0 + gate * (1.0 - sig))).astype(BF16)
    up_delta = (hidden_grad * silu).astype(BF16)
    mine = jnp.concatenate([hidden, gate_delta, up_delta], axis=1)
    own = spread(mine, "z", nz).reshape(half, 3 * h)
    other = lax.ppermute(own, "core", swap)
    blocks = output_blocks(core, own, other, *weights)
    layer_out, input_grad = totals(lax.all_to_all(blocks, ("x", "y"), 0, 0))

    hid, gd, ud = (jnp.concatenate([own[:, i * h : (i + 1) * h], other[:, i * h : (i + 1) * h]], axis=0) for i in range(3))
    x_cat = jnp.concatenate([x_own, x_other], axis=0)
    g_cat = jnp.concatenate([g_own, g_other], axis=0)
    return layer_out, input_grad, t_mm(x_cat, gd), t_mm(x_cat, ud), t_mm(hid, g_cat)


def solution(mesh):
    sizes = (8, 4, 8, 2)
    fine = Mesh(mesh.devices.reshape(sizes), ("y", "x", "z", "core"))
    tokens, features = ("y", "x"), ("z", "core")
    tile = P(tokens, features)
    return jax.shard_map(
        functools.partial(local, sizes),
        mesh=fine,
        in_specs=(tile, P(features, tokens), P(features, tokens), tile, tile),
        out_specs=(tile, tile, P(features, tokens), P(features, tokens), tile),
        check_vma=False,
    )
```

```python
import functools

import jax
import jax.numpy as jnp
from jax import lax
from jax.experimental import pallas as pl
from jax.experimental.pallas import tpu as pltpu
from jax.sharding import Mesh, PartitionSpec as P

F32 = jnp.float32
BF16 = jnp.bfloat16
VM = pl.BlockSpec(memory_space=pltpu.VMEM)
SM = pl.BlockSpec(memory_space=pltpu.SMEM)
PARAMS = pltpu.CompilerParams(vmem_limit_bytes=40 * 2**20)


def mm(left, right):
    return jnp.dot(left, right, preferred_element_type=F32)


def mm_t(left, right):
    return lax.dot_general(left, right, (((1,), (1,)), ((), ())), preferred_element_type=F32)


def t_mm(left, right):
    return lax.dot_general(left, right, (((0,), (0,)), ((), ())), preferred_element_type=F32)


def spread(block, axis, size):
    return lax.all_to_all(jnp.broadcast_to(block[None], (size,) + block.shape), axis, 0, 0)


def add_up(blocks):
    total = blocks[0].astype(F32)
    for i in range(1, blocks.shape[0]):
        total = total + blocks[i].astype(F32)
    return total


def low_rows(shape):
    return lax.broadcasted_iota(jnp.int32, shape, 1) < 4


def pack_kernel(both, out):
    first, middle, last = (both[i : i + 8].astype(F32) for i in (0, 8, 16))
    low = lax.broadcasted_iota(jnp.int32, first.shape, 0) < 4
    second = jnp.where(low, pltpu.roll(middle, 4, 0), pltpu.roll(last, 4, 0))
    tail = jnp.where(low, middle, last)
    for i in range(out.shape[0]):
        out[i, 0:8, :] = first.astype(BF16)
        out[i, 8:16, :] = second.astype(BF16)
        out[i, 16:24, :] = tail.astype(BF16)


def pack(a, b, copies):
    both = jnp.concatenate([a, b], axis=0)
    return pl.pallas_call(
        pack_kernel,
        out_shape=jax.ShapeDtypeStruct((copies,) + both.shape, BF16),
        in_specs=[VM],
        out_specs=VM,
        compiler_params=PARAMS,
        name="pack",
    )(both)


def total_kernel(blocks, layer_out, input_grad):
    total = blocks[0].astype(F32)
    for i in range(1, blocks.shape[0]):
        total = total + blocks[i].astype(F32)
    layer_out[:8] = total[:8].astype(BF16)
    layer_out[8:] = total[16:20].astype(BF16)
    input_grad[:8] = total[8:16].astype(BF16)
    input_grad[8:] = total[20:24].astype(BF16)


def totals(blocks):
    shape = jax.ShapeDtypeStruct((12, blocks.shape[2]), BF16)
    return pl.pallas_call(total_kernel, out_shape=(shape, shape), in_specs=[VM], compiler_params=PARAMS, name="totals")(blocks)


def partial_kernel(which, blocks, gate_weight, up_weight, down_weight, out, x_out, g_out):
    m = x_out.shape[0] // 12
    d = x_out.shape[1]
    rows = pl.ds(which[0] * m, m)
    tail = blocks[rows, 16:24, :].astype(F32).reshape(m // 2, 16, d)
    even, odd = tail[:, :8], tail[:, 8:]
    low = low_rows(even.shape)
    x_tail = jnp.where(low, even, pltpu.roll(odd, 4, 1)).reshape(m * 4, d)
    g_tail = jnp.where(low, pltpu.roll(even, 4, 1), odd).reshape(m * 4, d)
    x_head = blocks[rows, 0:8, :].astype(F32).reshape(m * 8, d)
    g_head = blocks[rows, 8:16, :].astype(F32).reshape(m * 8, d)
    x = jnp.concatenate([x_head, x_tail], axis=0).astype(BF16)
    g = jnp.concatenate([g_head, g_tail], axis=0).astype(BF16)
    x_out[...] = x
    g_out[...] = g
    h = gate_weight.shape[1]
    out[:, :h] = mm(x, gate_weight[...])
    out[:, h : 2 * h] = mm(x, up_weight[...])
    out[:, 2 * h :] = mm_t(g, down_weight[...])


def partial_sums(which, blocks, gate_weight, up_weight, down_weight):
    n = blocks.shape[0] * 12 // 2
    d = blocks.shape[2]
    h = gate_weight.shape[1]
    shape = jax.ShapeDtypeStruct
    return pl.pallas_call(
        partial_kernel,
        out_shape=(shape((n, 3 * h), F32), shape((n, d), BF16), shape((n, d), BF16)),
        in_specs=[SM, VM, VM, VM, VM],
        out_specs=(VM, VM, VM),
        compiler_params=PARAMS,
        cost_estimate=pl.CostEstimate(flops=2 * n * d * 3 * h, bytes_accessed=4 * n * 3 * h, transcendentals=0),
        name="partial_sums",
    )(which, blocks, gate_weight, up_weight, down_weight)


def output_kernel(which, part, gate_weight, up_weight, down_weight, *rest):
    out = rest[-1]
    h = gate_weight.shape[1]
    d = gate_weight.shape[0]
    m = out.shape[0]
    f = mm(part[:, :h], down_weight[...])
    b = mm_t(part[:, h : 2 * h], gate_weight[...]) + mm_t(part[:, 2 * h :], up_weight[...])
    out[:, 0:8, :] = f[: m * 8].reshape(m, 8, d).astype(BF16)
    out[:, 8:16, :] = b[: m * 8].reshape(m, 8, d).astype(BF16)
    f = f[m * 8 :].reshape(m // 2, 8, d)
    b = b[m * 8 :].reshape(m // 2, 8, d)
    low = low_rows(f.shape)
    even = jnp.where(low, f, pltpu.roll(b, 4, 1))
    odd = jnp.where(low, pltpu.roll(f, 4, 1), b)
    out[:, 16:24, :] = jnp.concatenate([even, odd], axis=1).reshape(m, 8, d).astype(BF16)


def output_blocks(which, part, weights, blocks=None):
    n, width = part.shape
    d = weights[0].shape[0]
    m = n // 12
    more = [] if blocks is None else [blocks]
    return pl.pallas_call(
        output_kernel,
        out_shape=jax.ShapeDtypeStruct((2 * m, 24, d), BF16),
        grid_spec=pltpu.PrefetchScalarGridSpec(
            num_scalar_prefetch=1,
            grid=(1,),
            in_specs=[VM, VM, VM, VM] + [pl.BlockSpec(memory_space=pl.ANY)] * len(more),
            out_specs=pl.BlockSpec((m, 24, d), lambda i, which: (which[0], 0, 0)),
        ),
        input_output_aliases={5: 0} if more else {},
        compiler_params=PARAMS,
        cost_estimate=pl.CostEstimate(flops=2 * n * d * width, bytes_accessed=4 * n * d, transcendentals=0),
        name="output_blocks",
    )(which, part, *weights, *more)


def local(sizes, activations, gate_weight, up_weight, down_weight, out_grad):
    ny, nx, nz, nc = sizes
    d = activations.shape[1]
    h = gate_weight.shape[1]
    rows = ny * nx
    swap = [(0, 1), (1, 0)]
    core = lax.axis_index("core").astype(jnp.int32).reshape(1)
    away = 1 - core

    both = pack(activations, out_grad, ny)
    both, core, away = lax.optimization_barrier((both, core, away))
    both = spread(lax.all_to_all(both, "y", 0, 0), "x", nx).reshape(rows, 24, d)
    weights = (gate_weight, up_weight, down_weight)
    send, x_other, g_other = partial_sums(away, both, *weights)
    sent = lax.ppermute(send, "core", swap)
    keep, x_own, g_own = partial_sums(core, both, *weights)
    half = keep.shape[0]
    n = half // nz
    chip = (keep + sent).astype(BF16).reshape(nz, n, 3 * h)
    summed = add_up(lax.all_to_all(chip, "z", 0, 0))
    gate, up, hidden_grad = summed[:, :h], summed[:, h : 2 * h], summed[:, 2 * h :]
    sig = jax.nn.sigmoid(gate)
    silu = gate * sig
    hidden = (silu * up).astype(BF16)
    gate_delta = (hidden_grad * up * sig * (1.0 + gate * (1.0 - sig))).astype(BF16)
    up_delta = (hidden_grad * silu).astype(BF16)
    mine = jnp.concatenate([hidden, gate_delta, up_delta], axis=1)
    own = spread(mine, "z", nz).reshape(half, 3 * h)
    other = lax.ppermute(own, "core", swap)
    blocks = output_blocks(core, own, weights)
    blocks = output_blocks(away, other, weights, blocks)
    layer_out, input_grad = totals(lax.all_to_all(blocks, ("x", "y"), 0, 0))

    hid, gd, ud = (jnp.concatenate([own[:, i * h : (i + 1) * h], other[:, i * h : (i + 1) * h]], axis=0) for i in range(3))
    x_cat = jnp.concatenate([x_own, x_other], axis=0)
    g_cat = jnp.concatenate([g_own, g_other], axis=0)
    return layer_out, input_grad, t_mm(x_cat, gd), t_mm(x_cat, ud), t_mm(hid, g_cat)


def solution(mesh):
    sizes = (8, 4, 8, 2)
    fine = Mesh(mesh.devices.reshape(sizes), ("y", "x", "z", "core"))
    tokens, features = ("y", "x"), ("z", "core")
    tile = P(tokens, features)
    return jax.shard_map(
        functools.partial(local, sizes),
        mesh=fine,
        in_specs=(tile, P(features, tokens), P(features, tokens), tile, tile),
        out_specs=(tile, tile, P(features, tokens), P(features, tokens), tile),
        check_vma=False,
    )
```

```python
import functools

import jax
import jax.numpy as jnp
from jax import lax
from jax.experimental import pallas as pl
from jax.experimental.pallas import tpu as pltpu
from jax.sharding import Mesh, PartitionSpec as P

F32 = jnp.float32
BF16 = jnp.bfloat16
VM = pl.BlockSpec(memory_space=pltpu.VMEM)
SM = pl.BlockSpec(memory_space=pltpu.SMEM)
PARAMS = pltpu.CompilerParams(vmem_limit_bytes=40 * 2**20)


def mm(left, right):
    return jnp.dot(left, right, preferred_element_type=F32)


def mm_t(left, right):
    return lax.dot_general(left, right, (((1,), (1,)), ((), ())), preferred_element_type=F32)


def t_mm(left, right):
    return lax.dot_general(left, right, (((0,), (0,)), ((), ())), preferred_element_type=F32)


def spread(block, axis, size):
    return lax.all_to_all(jnp.broadcast_to(block[None], (size,) + block.shape), axis, 0, 0)


def add_up(blocks):
    total = blocks[0].astype(F32)
    for i in range(1, blocks.shape[0]):
        total = total + blocks[i].astype(F32)
    return total


def low_rows(shape):
    return lax.broadcasted_iota(jnp.int32, shape, 1) < 4


def pack_kernel(both, out):
    first, middle, last = (both[i : i + 8].astype(F32) for i in (0, 8, 16))
    low = lax.broadcasted_iota(jnp.int32, first.shape, 0) < 4
    second = jnp.where(low, pltpu.roll(middle, 4, 0), pltpu.roll(last, 4, 0))
    tail = jnp.where(low, middle, last)
    for i in range(out.shape[0]):
        out[i, 0:8, :] = first.astype(BF16)
        out[i, 8:16, :] = second.astype(BF16)
        out[i, 16:24, :] = tail.astype(BF16)


def pack(a, b, copies):
    both = jnp.concatenate([a, b], axis=0)
    return pl.pallas_call(
        pack_kernel,
        out_shape=jax.ShapeDtypeStruct((copies,) + both.shape, BF16),
        in_specs=[VM],
        out_specs=VM,
        compiler_params=PARAMS,
        name="pack",
    )(both)


def total_kernel(blocks, layer_out, input_grad):
    total = blocks[0].astype(F32)
    for i in range(1, blocks.shape[0]):
        total = total + blocks[i].astype(F32)
    layer_out[:8] = total[:8].astype(BF16)
    layer_out[8:] = total[16:20].astype(BF16)
    input_grad[:8] = total[8:16].astype(BF16)
    input_grad[8:] = total[20:24].astype(BF16)


def totals(blocks):
    shape = jax.ShapeDtypeStruct((12, blocks.shape[2]), BF16)
    return pl.pallas_call(total_kernel, out_shape=(shape, shape), in_specs=[VM], compiler_params=PARAMS, name="totals")(blocks)


def unpack(blocks, rows):
    m, d = rows.size, blocks.shape[2]
    tail = blocks[rows, 16:24, :].astype(F32).reshape(m // 2, 16, d)
    even, odd = tail[:, :8], tail[:, 8:]
    low = low_rows(even.shape)
    a_tail = jnp.where(low, even, pltpu.roll(odd, 4, 1)).reshape(m * 4, d)
    b_tail = jnp.where(low, pltpu.roll(even, 4, 1), odd).reshape(m * 4, d)
    a_head = blocks[rows, 0:8, :].astype(F32).reshape(m * 8, d)
    b_head = blocks[rows, 8:16, :].astype(F32).reshape(m * 8, d)
    a = jnp.concatenate([a_head, a_tail], axis=0).astype(BF16)
    b = jnp.concatenate([b_head, b_tail], axis=0).astype(BF16)
    return a, b


def near_kernel(which, blocks, gate_weight, up_weight, down_weight, out, x_all, g_all):
    m = blocks.shape[0] // 2
    n = x_all.shape[0] // 2
    h = gate_weight.shape[1]
    x, g = unpack(blocks, pl.ds(which[0] * m, m))
    x_all[:n], g_all[:n] = x, g
    out[:, :h] = mm(x, gate_weight[...])
    out[:, h : 2 * h] = mm(x, up_weight[...])
    out[:, 2 * h :] = mm_t(g, down_weight[...])
    x_all[n:], g_all[n:] = unpack(blocks, pl.ds((1 - which[0]) * m, m))


def near_sums(which, blocks, weights):
    n = blocks.shape[0] * 12
    d = blocks.shape[2]
    h = weights[0].shape[1]
    shape = jax.ShapeDtypeStruct
    return pl.pallas_call(
        near_kernel,
        out_shape=(shape((n // 2, 3 * h), F32), shape((n, d), BF16), shape((n, d), BF16)),
        in_specs=[SM, VM, VM, VM, VM],
        out_specs=(VM, VM, VM),
        compiler_params=PARAMS,
        cost_estimate=pl.CostEstimate(flops=3 * n * d * h, bytes_accessed=6 * n * h, transcendentals=0),
        name="near_sums",
    )(which, blocks, *weights)


def far_kernel(near, blocks, gate_weight, up_weight, down_weight, out):
    h = gate_weight.shape[1]
    x, g = unpack(blocks, pl.ds(0, blocks.shape[0]))
    out[:, :h] = (near[:, :h] + mm(x, gate_weight[...])).astype(BF16)
    out[:, h : 2 * h] = (near[:, h : 2 * h] + mm(x, up_weight[...])).astype(BF16)
    out[:, 2 * h :] = (near[:, 2 * h :] + mm_t(g, down_weight[...])).astype(BF16)


def far_sums(near, blocks, weights):
    n, width = near.shape
    return pl.pallas_call(
        far_kernel,
        out_shape=jax.ShapeDtypeStruct(near.shape, BF16),
        in_specs=[VM, VM, VM, VM, VM],
        out_specs=VM,
        compiler_params=PARAMS,
        cost_estimate=pl.CostEstimate(flops=2 * n * width * blocks.shape[2], bytes_accessed=6 * n * width, transcendentals=0),
        name="far_sums",
    )(near, blocks, *weights)


def output_kernel(which, part, gate_weight, up_weight, down_weight, *rest):
    out = rest[-1]
    h = gate_weight.shape[1]
    d = gate_weight.shape[0]
    m = out.shape[0]
    f = mm(part[:, :h], down_weight[...])
    b = mm_t(part[:, h : 2 * h], gate_weight[...]) + mm_t(part[:, 2 * h :], up_weight[...])
    out[:, 0:8, :] = f[: m * 8].reshape(m, 8, d).astype(BF16)
    out[:, 8:16, :] = b[: m * 8].reshape(m, 8, d).astype(BF16)
    f = f[m * 8 :].reshape(m // 2, 8, d)
    b = b[m * 8 :].reshape(m // 2, 8, d)
    low = low_rows(f.shape)
    even = jnp.where(low, f, pltpu.roll(b, 4, 1))
    odd = jnp.where(low, pltpu.roll(f, 4, 1), b)
    out[:, 16:24, :] = jnp.concatenate([even, odd], axis=1).reshape(m, 8, d).astype(BF16)


def output_blocks(which, part, weights, blocks=None):
    n, width = part.shape
    d = weights[0].shape[0]
    m = n // 12
    more = [] if blocks is None else [blocks]
    return pl.pallas_call(
        output_kernel,
        out_shape=jax.ShapeDtypeStruct((2 * m, 24, d), BF16),
        grid_spec=pltpu.PrefetchScalarGridSpec(
            num_scalar_prefetch=1,
            grid=(1,),
            in_specs=[VM, VM, VM, VM] + [pl.BlockSpec(memory_space=pl.ANY)] * len(more),
            out_specs=pl.BlockSpec((m, 24, d), lambda i, which: (which[0], 0, 0)),
        ),
        input_output_aliases={5: 0} if more else {},
        compiler_params=PARAMS,
        cost_estimate=pl.CostEstimate(flops=2 * n * d * width, bytes_accessed=4 * n * d, transcendentals=0),
        name="output_blocks",
    )(which, part, *weights, *more)


def local(sizes, activations, gate_weight, up_weight, down_weight, out_grad):
    ny, nx, nz, nc = sizes
    d = activations.shape[1]
    h = gate_weight.shape[1]
    rows = ny * nx
    swap = [(0, 1), (1, 0)]
    core = lax.axis_index("core").astype(jnp.int32).reshape(1)
    away = 1 - core

    both = pack(activations, out_grad, ny)
    both, core, away = lax.optimization_barrier((both, core, away))
    weights = (gate_weight, up_weight, down_weight)
    column = lax.all_to_all(both, "y", 0, 0)
    column, *moving = lax.optimization_barrier((column, *weights))
    far_weights = [lax.ppermute(w, "core", swap) for w in moving]
    both = spread(column, "x", nx).reshape(rows, 24, d)
    theirs = lax.dynamic_slice_in_dim(both, away[0] * (rows // nc), rows // nc, axis=0)
    far = lax.ppermute(theirs, "core", swap)
    near, x_cat, g_cat = near_sums(core, both, weights)
    half = near.shape[0]
    n = half // nz
    chip = far_sums(near, far, far_weights).reshape(nz, n, 3 * h)
    summed = add_up(lax.all_to_all(chip, "z", 0, 0))
    gate, up, hidden_grad = summed[:, :h], summed[:, h : 2 * h], summed[:, 2 * h :]
    sig = jax.nn.sigmoid(gate)
    silu = gate * sig
    hidden = (silu * up).astype(BF16)
    gate_delta = (hidden_grad * up * sig * (1.0 + gate * (1.0 - sig))).astype(BF16)
    up_delta = (hidden_grad * silu).astype(BF16)
    mine = jnp.concatenate([hidden, gate_delta, up_delta], axis=1)
    own = spread(mine, "z", nz).reshape(half, 3 * h)
    other = lax.ppermute(own, "core", swap)
    blocks = output_blocks(core, own, weights)
    blocks = output_blocks(away, other, weights, blocks)
    layer_out, input_grad = totals(lax.all_to_all(blocks, ("x", "y"), 0, 0))

    hid, gd, ud = (jnp.concatenate([own[:, i * h : (i + 1) * h], other[:, i * h : (i + 1) * h]], axis=0) for i in range(3))
    return layer_out, input_grad, t_mm(x_cat, gd), t_mm(x_cat, ud), t_mm(hid, g_cat)


def solution(mesh):
    sizes = (8, 4, 8, 2)
    fine = Mesh(mesh.devices.reshape(sizes), ("y", "x", "z", "core"))
    tokens, features = ("y", "x"), ("z", "core")
    tile = P(tokens, features)
    return jax.shard_map(
        functools.partial(local, sizes),
        mesh=fine,
        in_specs=(tile, P(features, tokens), P(features, tokens), tile, tile),
        out_specs=(tile, tile, P(features, tokens), P(features, tokens), tile),
        check_vma=False,
    )
```

```python
import functools

import jax
import jax.numpy as jnp
from jax import lax
from jax.experimental import pallas as pl
from jax.experimental.pallas import tpu as pltpu
from jax.sharding import Mesh, PartitionSpec as P

F32 = jnp.float32
BF16 = jnp.bfloat16
VM = pl.BlockSpec(memory_space=pltpu.VMEM)
SM = pl.BlockSpec(memory_space=pltpu.SMEM)
PARAMS = pltpu.CompilerParams(vmem_limit_bytes=40 * 2**20)


def mm(left, right):
    return jnp.dot(left, right, preferred_element_type=F32)


def mm_t(left, right):
    return lax.dot_general(left, right, (((1,), (1,)), ((), ())), preferred_element_type=F32)


def t_mm(left, right):
    return lax.dot_general(left, right, (((0,), (0,)), ((), ())), preferred_element_type=F32)


def spread(block, axis, size):
    return lax.all_to_all(jnp.broadcast_to(block[None], (size,) + block.shape), axis, 0, 0)


def add_up(blocks):
    total = blocks[0].astype(F32)
    for i in range(1, blocks.shape[0]):
        total = total + blocks[i].astype(F32)
    return total


def low_rows(shape):
    return lax.broadcasted_iota(jnp.int32, shape, 1) < 4


def pack_kernel(both, out):
    first, middle, last = (both[i : i + 8].astype(F32) for i in (0, 8, 16))
    low = lax.broadcasted_iota(jnp.int32, first.shape, 0) < 4
    second = jnp.where(low, pltpu.roll(middle, 4, 0), pltpu.roll(last, 4, 0))
    tail = jnp.where(low, middle, last)
    for i in range(out.shape[0]):
        out[i, 0:8, :] = first.astype(BF16)
        out[i, 8:16, :] = second.astype(BF16)
        out[i, 16:24, :] = tail.astype(BF16)


def pack(a, b, copies):
    both = jnp.concatenate([a, b], axis=0)
    return pl.pallas_call(
        pack_kernel,
        out_shape=jax.ShapeDtypeStruct((copies,) + both.shape, BF16),
        in_specs=[VM],
        out_specs=VM,
        compiler_params=PARAMS,
        name="pack",
    )(both)


def fan_kernel(block, out, sems):
    copies = [pltpu.make_async_copy(block, out.at[i], sems.at[i]) for i in range(out.shape[0])]
    for copy in copies:
        copy.start()
    for copy in copies:
        copy.wait()


def fan(block, copies):
    return pl.pallas_call(
        fan_kernel,
        out_shape=jax.ShapeDtypeStruct((copies,) + block.shape, BF16),
        in_specs=[VM],
        out_specs=pl.BlockSpec(memory_space=pl.ANY),
        scratch_shapes=[pltpu.SemaphoreType.DMA((copies,))],
        compiler_params=PARAMS,
        name="fan",
    )(block)


def total_kernel(blocks, layer_out, input_grad):
    total = blocks[0].astype(F32)
    for i in range(1, blocks.shape[0]):
        total = total + blocks[i].astype(F32)
    layer_out[:8] = total[:8].astype(BF16)
    layer_out[8:] = total[16:20].astype(BF16)
    input_grad[:8] = total[8:16].astype(BF16)
    input_grad[8:] = total[20:24].astype(BF16)


def totals(blocks):
    shape = jax.ShapeDtypeStruct((12, blocks.shape[2]), BF16)
    return pl.pallas_call(total_kernel, out_shape=(shape, shape), in_specs=[VM], compiler_params=PARAMS, name="totals")(blocks)


def unpack(blocks, rows):
    m, d = rows.size, blocks.shape[2]
    tail = blocks[rows, 16:24, :].astype(F32).reshape(m // 2, 16, d)
    even, odd = tail[:, :8], tail[:, 8:]
    low = low_rows(even.shape)
    a_tail = jnp.where(low, even, pltpu.roll(odd, 4, 1)).reshape(m * 4, d)
    b_tail = jnp.where(low, pltpu.roll(even, 4, 1), odd).reshape(m * 4, d)
    a_head = blocks[rows, 0:8, :].astype(F32).reshape(m * 8, d)
    b_head = blocks[rows, 8:16, :].astype(F32).reshape(m * 8, d)
    a = jnp.concatenate([a_head, a_tail], axis=0).astype(BF16)
    b = jnp.concatenate([b_head, b_tail], axis=0).astype(BF16)
    return a, b


def near_kernel(which, blocks, gate_weight, up_weight, down_weight, out, x_all, g_all):
    m = blocks.shape[0] // 2
    n = x_all.shape[0] // 2
    h = gate_weight.shape[1]
    x, g = unpack(blocks, pl.ds(which[0] * m, m))
    x_all[:n], g_all[:n] = x, g
    out[:, :h] = mm(x, gate_weight[...])
    out[:, h : 2 * h] = mm(x, up_weight[...])
    out[:, 2 * h :] = mm_t(g, down_weight[...])
    x_all[n:], g_all[n:] = unpack(blocks, pl.ds((1 - which[0]) * m, m))


def near_sums(which, blocks, weights):
    n = blocks.shape[0] * 12
    d = blocks.shape[2]
    h = weights[0].shape[1]
    shape = jax.ShapeDtypeStruct
    return pl.pallas_call(
        near_kernel,
        out_shape=(shape((n // 2, 3 * h), F32), shape((n, d), BF16), shape((n, d), BF16)),
        in_specs=[SM, VM, VM, VM, VM],
        out_specs=(VM, VM, VM),
        compiler_params=PARAMS,
        cost_estimate=pl.CostEstimate(flops=3 * n * d * h, bytes_accessed=6 * n * h, transcendentals=0),
        name="near_sums",
    )(which, blocks, *weights)


def far_kernel(near, blocks, gate_weight, up_weight, down_in, out, down_weight, sem):
    fetch = pltpu.make_async_copy(down_in, down_weight, sem)
    fetch.start()
    h = gate_weight.shape[1]
    x, g = unpack(blocks, pl.ds(0, blocks.shape[0]))
    out[:, :h] = (near[:, :h] + mm(x, gate_weight[...])).astype(BF16)
    out[:, h : 2 * h] = (near[:, h : 2 * h] + mm(x, up_weight[...])).astype(BF16)
    fetch.wait()
    out[:, 2 * h :] = (near[:, 2 * h :] + mm_t(g, down_weight[...])).astype(BF16)


def far_sums(near, blocks, weights):
    n, width = near.shape
    return pl.pallas_call(
        far_kernel,
        out_shape=jax.ShapeDtypeStruct(near.shape, BF16),
        in_specs=[VM, VM, VM, VM, pl.BlockSpec(memory_space=pl.ANY)],
        out_specs=VM,
        scratch_shapes=[pltpu.VMEM(weights[2].shape, BF16), pltpu.SemaphoreType.DMA],
        compiler_params=PARAMS,
        cost_estimate=pl.CostEstimate(flops=2 * n * width * blocks.shape[2], bytes_accessed=6 * n * width, transcendentals=0),
        name="far_sums",
    )(near, blocks, *weights)


def output_kernel(which, part, gate_weight, up_weight, down_weight, *rest):
    out = rest[-1]
    h = gate_weight.shape[1]
    d = gate_weight.shape[0]
    m = out.shape[0]
    f = mm(part[:, :h], down_weight[...])
    b = mm_t(part[:, h : 2 * h], gate_weight[...]) + mm_t(part[:, 2 * h :], up_weight[...])
    out[:, 0:8, :] = f[: m * 8].reshape(m, 8, d).astype(BF16)
    out[:, 8:16, :] = b[: m * 8].reshape(m, 8, d).astype(BF16)
    f = f[m * 8 :].reshape(m // 2, 8, d)
    b = b[m * 8 :].reshape(m // 2, 8, d)
    low = low_rows(f.shape)
    even = jnp.where(low, f, pltpu.roll(b, 4, 1))
    odd = jnp.where(low, pltpu.roll(f, 4, 1), b)
    out[:, 16:24, :] = jnp.concatenate([even, odd], axis=1).reshape(m, 8, d).astype(BF16)


def output_blocks(which, part, weights, blocks=None):
    n, width = part.shape
    d = weights[0].shape[0]
    m = n // 12
    more = [] if blocks is None else [blocks]
    return pl.pallas_call(
        output_kernel,
        out_shape=jax.ShapeDtypeStruct((2 * m, 24, d), BF16),
        grid_spec=pltpu.PrefetchScalarGridSpec(
            num_scalar_prefetch=1,
            grid=(1,),
            in_specs=[VM, VM, VM, VM] + [pl.BlockSpec(memory_space=pl.ANY)] * len(more),
            out_specs=pl.BlockSpec((m, 24, d), lambda i, which: (which[0], 0, 0)),
        ),
        input_output_aliases={5: 0} if more else {},
        compiler_params=PARAMS,
        cost_estimate=pl.CostEstimate(flops=2 * n * d * width, bytes_accessed=4 * n * d, transcendentals=0),
        name="output_blocks",
    )(which, part, *weights, *more)


def local(sizes, activations, gate_weight, up_weight, down_weight, out_grad):
    ny, nx, nz, nc = sizes
    d = activations.shape[1]
    h = gate_weight.shape[1]
    rows = ny * nx
    swap = [(0, 1), (1, 0)]
    core = lax.axis_index("core").astype(jnp.int32).reshape(1)
    away = 1 - core

    both = pack(activations, out_grad, ny)
    both, core, away = lax.optimization_barrier((both, core, away))
    weights = (gate_weight, up_weight, down_weight)
    column = lax.all_to_all(both, "y", 0, 0)
    column, *moving = lax.optimization_barrier((column, *weights))
    far_weights = [lax.ppermute(w, "core", swap) for w in moving]
    both = lax.all_to_all(fan(column, nx), "x", 0, 0).reshape(rows, 24, d)
    both, far_weights = lax.optimization_barrier((both, far_weights))
    theirs = lax.dynamic_slice_in_dim(both, away[0] * (rows // nc), rows // nc, axis=0)
    far = lax.ppermute(theirs, "core", swap)
    near, x_cat, g_cat = near_sums(core, both, weights)
    half = near.shape[0]
    n = half // nz
    chip = far_sums(near, far, far_weights).reshape(nz, n, 3 * h)
    summed = add_up(lax.all_to_all(chip, "z", 0, 0))
    gate, up, hidden_grad = summed[:, :h], summed[:, h : 2 * h], summed[:, 2 * h :]
    sig = jax.nn.sigmoid(gate)
    silu = gate * sig
    hidden = (silu * up).astype(BF16)
    gate_delta = (hidden_grad * up * sig * (1.0 + gate * (1.0 - sig))).astype(BF16)
    up_delta = (hidden_grad * silu).astype(BF16)
    mine = jnp.concatenate([hidden, gate_delta, up_delta], axis=1)
    own = spread(mine, "z", nz).reshape(half, 3 * h)
    other = lax.ppermute(own, "core", swap)
    blocks = output_blocks(core, own, weights)
    blocks = output_blocks(away, other, weights, blocks)
    layer_out, input_grad = totals(lax.all_to_all(blocks, ("x", "y"), 0, 0))

    hid, gd, ud = (jnp.concatenate([own[:, i * h : (i + 1) * h], other[:, i * h : (i + 1) * h]], axis=0) for i in range(3))
    return layer_out, input_grad, t_mm(x_cat, gd), t_mm(x_cat, ud), t_mm(hid, g_cat)


def solution(mesh):
    sizes = (8, 4, 8, 2)
    fine = Mesh(mesh.devices.reshape(sizes), ("y", "x", "z", "core"))
    tokens, features = ("y", "x"), ("z", "core")
    tile = P(tokens, features)
    return jax.shard_map(
        functools.partial(local, sizes),
        mesh=fine,
        in_specs=(tile, P(features, tokens), P(features, tokens), tile, tile),
        out_specs=(tile, tile, P(features, tokens), P(features, tokens), tile),
        check_vma=False,
    )
```

```python
import functools

import jax
import jax.numpy as jnp
from jax import lax
from jax.experimental import pallas as pl
from jax.experimental.pallas import tpu as pltpu
from jax.sharding import Mesh, PartitionSpec as P

F32 = jnp.float32
BF16 = jnp.bfloat16
VM = pl.BlockSpec(memory_space=pltpu.VMEM)
SM = pl.BlockSpec(memory_space=pltpu.SMEM)
PARAMS = pltpu.CompilerParams(vmem_limit_bytes=40 * 2**20)


def mm(left, right):
    return jnp.dot(left, right, preferred_element_type=F32)


def mm_t(left, right):
    return lax.dot_general(left, right, (((1,), (1,)), ((), ())), preferred_element_type=F32)


def t_mm(left, right):
    return lax.dot_general(left, right, (((0,), (0,)), ((), ())), preferred_element_type=F32)


def spread(block, axis, size):
    return lax.all_to_all(jnp.broadcast_to(block[None], (size,) + block.shape), axis, 0, 0)


def add_up(blocks):
    total = blocks[0].astype(F32)
    for i in range(1, blocks.shape[0]):
        total = total + blocks[i].astype(F32)
    return total


def low_rows(shape):
    return lax.broadcasted_iota(jnp.int32, shape, 1) < 4


def pack_kernel(both, out):
    first, middle, last = (both[i : i + 8].astype(F32) for i in (0, 8, 16))
    low = lax.broadcasted_iota(jnp.int32, first.shape, 0) < 4
    second = jnp.where(low, pltpu.roll(middle, 4, 0), pltpu.roll(last, 4, 0))
    tail = jnp.where(low, middle, last)
    for i in range(out.shape[0]):
        out[i, 0:8, :] = first.astype(BF16)
        out[i, 8:16, :] = second.astype(BF16)
        out[i, 16:24, :] = tail.astype(BF16)


def pack(a, b, copies):
    both = jnp.concatenate([a, b], axis=0)
    return pl.pallas_call(
        pack_kernel,
        out_shape=jax.ShapeDtypeStruct((copies,) + both.shape, BF16),
        in_specs=[VM],
        out_specs=VM,
        compiler_params=PARAMS,
        name="pack",
    )(both)


def total_kernel(blocks, layer_out, input_grad):
    total = blocks[0].astype(F32)
    for i in range(1, blocks.shape[0]):
        total = total + blocks[i].astype(F32)
    layer_out[:8] = total[:8].astype(BF16)
    layer_out[8:] = total[16:20].astype(BF16)
    input_grad[:8] = total[8:16].astype(BF16)
    input_grad[8:] = total[20:24].astype(BF16)


def totals(blocks):
    shape = jax.ShapeDtypeStruct((12, blocks.shape[2]), BF16)
    return pl.pallas_call(total_kernel, out_shape=(shape, shape), in_specs=[VM], compiler_params=PARAMS, name="totals")(blocks)


def partial_kernel(which, blocks, gate_weight, up_weight, down_weight, out, x_out, g_out):
    m = x_out.shape[0] // 12
    d = x_out.shape[1]
    rows = pl.ds(which[0] * m, m)
    tail = blocks[rows, 16:24, :].astype(F32).reshape(m // 2, 16, d)
    even, odd = tail[:, :8], tail[:, 8:]
    low = low_rows(even.shape)
    x_tail = jnp.where(low, even, pltpu.roll(odd, 4, 1)).reshape(m * 4, d)
    g_tail = jnp.where(low, pltpu.roll(even, 4, 1), odd).reshape(m * 4, d)
    x_head = blocks[rows, 0:8, :].astype(F32).reshape(m * 8, d)
    g_head = blocks[rows, 8:16, :].astype(F32).reshape(m * 8, d)
    x = jnp.concatenate([x_head, x_tail], axis=0).astype(BF16)
    g = jnp.concatenate([g_head, g_tail], axis=0).astype(BF16)
    x_out[...] = x
    g_out[...] = g
    h = gate_weight.shape[1]
    out[:, :h] = mm(x, gate_weight[...])
    out[:, h : 2 * h] = mm(x, up_weight[...])
    out[:, 2 * h :] = mm_t(g, down_weight[...])


def partial_sums(which, blocks, gate_weight, up_weight, down_weight):
    n = blocks.shape[0] * 12 // 2
    d = blocks.shape[2]
    h = gate_weight.shape[1]
    shape = jax.ShapeDtypeStruct
    return pl.pallas_call(
        partial_kernel,
        out_shape=(shape((n, 3 * h), F32), shape((n, d), BF16), shape((n, d), BF16)),
        in_specs=[SM, VM, VM, VM, VM],
        out_specs=(VM, VM, VM),
        compiler_params=PARAMS,
        cost_estimate=pl.CostEstimate(flops=2 * n * d * 3 * h, bytes_accessed=4 * n * 3 * h, transcendentals=0),
        name="partial_sums",
    )(which, blocks, gate_weight, up_weight, down_weight)


def output_kernel(which, part, gate_weight, up_weight, down_weight, *rest):
    out = rest[-1]
    h = gate_weight.shape[1]
    d = gate_weight.shape[0]
    ny, nx = out.shape[:2]
    m = ny * nx
    f = mm(part[:, :h], down_weight[...])
    b = mm_t(part[:, h : 2 * h], gate_weight[...]) + mm_t(part[:, 2 * h :], up_weight[...])
    f_head = f[: m * 8].reshape(m, 8, d).astype(BF16)
    b_head = b[: m * 8].reshape(m, 8, d).astype(BF16)
    f = f[m * 8 :].reshape(m // 2, 8, d)
    b = b[m * 8 :].reshape(m // 2, 8, d)
    low = low_rows(f.shape)
    even = jnp.where(low, f, pltpu.roll(b, 4, 1))
    odd = jnp.where(low, pltpu.roll(f, 4, 1), b)
    tail = jnp.concatenate([even, odd], axis=1).reshape(m, 8, d).astype(BF16)
    for x in range(nx):
        rows = slice(x * ny, (x + 1) * ny)
        out[:, x, 0:8, :] = f_head[rows]
        out[:, x, 8:16, :] = b_head[rows]
        out[:, x, 16:24, :] = tail[rows]


def output_blocks(which, part, weights, ny, blocks=None):
    n, width = part.shape
    d = weights[0].shape[0]
    nx = n // 12 // ny
    more = [] if blocks is None else [blocks]
    return pl.pallas_call(
        output_kernel,
        out_shape=jax.ShapeDtypeStruct((ny, 2 * nx, 24, d), BF16),
        grid_spec=pltpu.PrefetchScalarGridSpec(
            num_scalar_prefetch=1,
            grid=(1,),
            in_specs=[VM, VM, VM, VM] + [pl.BlockSpec(memory_space=pl.ANY)] * len(more),
            out_specs=pl.BlockSpec((ny, nx, 24, d), lambda i, which: (0, which[0], 0, 0)),
        ),
        input_output_aliases={5: 0} if more else {},
        compiler_params=PARAMS,
        cost_estimate=pl.CostEstimate(flops=2 * n * d * width, bytes_accessed=4 * n * d, transcendentals=0),
        name="output_blocks",
    )(which, part, *weights, *more)


def local(sizes, activations, gate_weight, up_weight, down_weight, out_grad):
    ny, nx, nz, nc = sizes
    d = activations.shape[1]
    h = gate_weight.shape[1]
    rows = ny * nx
    swap = [(0, 1), (1, 0)]
    core = lax.axis_index("core").astype(jnp.int32).reshape(1)
    away = 1 - core

    both = pack(activations, out_grad, ny)
    both, core, away = lax.optimization_barrier((both, core, away))
    both = spread(lax.all_to_all(both, "y", 0, 0), "x", nx).reshape(rows, 24, d)
    weights = (gate_weight, up_weight, down_weight)
    send, x_other, g_other = partial_sums(away, both, *weights)
    sent = lax.ppermute(send, "core", swap)
    keep, x_own, g_own = partial_sums(core, both, *weights)
    half = keep.shape[0]
    n = half // nz
    chip = (keep + sent).astype(BF16).reshape(nz, n, 3 * h)
    summed = add_up(lax.all_to_all(chip, "z", 0, 0))
    gate, up, hidden_grad = summed[:, :h], summed[:, h : 2 * h], summed[:, 2 * h :]
    sig = jax.nn.sigmoid(gate)
    silu = gate * sig
    hidden = (silu * up).astype(BF16)
    gate_delta = (hidden_grad * up * sig * (1.0 + gate * (1.0 - sig))).astype(BF16)
    up_delta = (hidden_grad * silu).astype(BF16)
    mine = jnp.concatenate([hidden, gate_delta, up_delta], axis=1)
    own = spread(mine, "z", nz).reshape(half, 3 * h)
    other = lax.ppermute(own, "core", swap)
    blocks = output_blocks(core, own, weights, ny)
    blocks = output_blocks(away, other, weights, ny, blocks).reshape(rows, 24, d)
    layer_out, input_grad = totals(lax.all_to_all(blocks, ("y", "x"), 0, 0))

    hid, gd, ud = (jnp.concatenate([own[:, i * h : (i + 1) * h], other[:, i * h : (i + 1) * h]], axis=0) for i in range(3))
    x_cat = jnp.concatenate([x_own, x_other], axis=0)
    g_cat = jnp.concatenate([g_own, g_other], axis=0)
    return layer_out, input_grad, t_mm(x_cat, gd), t_mm(x_cat, ud), t_mm(hid, g_cat)


def solution(mesh):
    sizes = (8, 4, 8, 2)
    fine = Mesh(mesh.devices.reshape(sizes), ("y", "x", "z", "core"))
    tokens, features = ("y", "x"), ("z", "core")
    tile = P(tokens, features)
    return jax.shard_map(
        functools.partial(local, sizes),
        mesh=fine,
        in_specs=(tile, P(features, tokens), P(features, tokens), tile, tile),
        out_specs=(tile, tile, P(features, tokens), P(features, tokens), tile),
        check_vma=False,
    )
```
